32 devices in a mesh: weight: 2 (over x), context: 4 (over y, core), tensor: 4 (over z).
Axes of the slice: x: 2, y: 2, z: 4, core: 2. Of those that a mesh axis runs over, the one named last changes fastest.
Arguments:
- layer_input: bfloat16 [1, 2048, 1024], P(None, ('weight', 'context')), may hold values from -6 to 6
- out_cotangent: bfloat16 [1, 2048, 1024], P(None, ('weight', 'context')), may hold values from -6 to 6
- input_gain: bfloat16 [1024], P('weight'), may hold values from 0.5 to 1.5
- mamba_gate: bfloat16 [1024, 1536], P('weight', 'tensor'), may hold values from -0.1875 to 0.1875
- mamba_value: bfloat16 [1024, 1536], P('weight', 'tensor'), may hold values from -0.1875 to 0.1875
- mamba_state: bfloat16 [1024, 256], P('weight'), may hold values from -0.1875 to 0.1875
- mamba_step: bfloat16 [1024, 24], P('weight', 'tensor'), may hold values from -0.1875 to 0.1875
- conv_value: float32 [4, 1536], P(None, 'tensor'), may hold values from -3 to 3
- conv_state: float32 [4, 256], replicated, may hold values from -3 to 3
- step_bias: float32 [24], P('tensor'), may hold values from -6.5 to -3
- decay_log: float32 [24], P('tensor'), may hold values from -1 to 0.7
- skip_gain: float32 [24], P('tensor'), may hold values from 0.5 to 1.5
- mixer_gain: float32 [1536], P('tensor'), may hold values from 0.5 to 1.5
- mamba_out: bfloat16 [1536, 1024], P('tensor', 'weight'), may hold values from -0.15625 to 0.15625
- query_weight: bfloat16 [1024, 512], P('weight', 'tensor'), may hold values from -6.5625 to 6.5625, as said below
- keys_values: bfloat16 [1024, 256], P('weight'), may hold values from -0.125 to 0.125, as said below
- attention_out: bfloat16 [512, 1024], P('tensor', 'weight'), may hold values from -2 to 2
- feed_gain: bfloat16 [1024], P('weight'), may hold values from 0.5 to 1.5
- feed_gate: bfloat16 [1024, 2048], P('weight', 'tensor'), may hold values from -0.1875 to 0.1875
- feed_up: bfloat16 [1024, 2048], P('weight', 'tensor'), may hold values from -0.1875 to 0.1875
- feed_down: bfloat16 [2048, 1024], P('tensor', 'weight'), may hold values from -0.125 to 0.125
Outputs:
- layer_output: bfloat16 [1, 2048, 1024], P(None, ('weight', 'context'))
- input_grad: float32 [1, 2048, 1024], P(None, ('weight', 'context'))
- input_gain_grad: float32 [1024], P('weight')
- mamba_gate_grad: float32 [1024, 1536], P('weight', 'tensor')
- mamba_value_grad: float32 [1024, 1536], P('weight', 'tensor')
- mamba_state_grad: float32 [1024, 256], P('weight')
- mamba_step_grad: float32 [1024, 24], P('weight', 'tensor')
- conv_value_grad: float32 [4, 1536], P(None, 'tensor')
- conv_state_grad: float32 [4, 256], replicated
- step_bias_grad: float32 [24], P('tensor')
- decay_log_grad: float32 [24], P('tensor')
- skip_gain_grad: float32 [24], P('tensor')
- mixer_gain_grad: float32 [1536], P('tensor')
- mamba_out_grad: float32 [1536, 1024], P('tensor', 'weight')
- query_weight_grad: float32 [1024, 512], P('weight', 'tensor')
- keys_values_grad: float32 [1024, 256], P('weight')
- attention_out_grad: float32 [512, 1024], P('tensor', 'weight')
- feed_gain_grad: float32 [1024], P('weight')
- feed_gate_grad: float32 [1024, 2048], P('weight', 'tensor')
- feed_up_grad: float32 [1024, 2048], P('weight', 'tensor')
- feed_down_grad: float32 [2048, 1024], P('tensor', 'weight')
The draws below stay inside these ranges and needn't reach their ends.
Inputs may be any that keep to these rules, and one draw needn't show every extreme that they name: `query_weight`: entries of the query projection lie within the range below. `keys_values`: entries of the key and value projection lie within the range below.
All inputs are finite; a program needn't handle non-finite values.
Results may differ from the reference program's by a relative error of at most 0.019.
The reference program's roundings to bfloat16 on the way (of `normed`, `mixer_in`, `normed_two`, `hidden`, `grad_mix`, `grad_att` and `grad_scores`) count: a program that leaves them out, or rounds other values in their place, can miss the bound.
Values may be sent and summed in bfloat16 or wider, within the bound.
No kernel may reach another device: no remote copies, remote signals or barrier semaphores. Data moves between devices by JAX's collectives and lax.ppermute only.
A program may use at most 128 MiB of HBM per device.

```python
import jax
import jax.numpy as jnp
from jax import lax

D = 1024
HEADS = 24
HEAD_DIM = 64
STATE = 128
CONV_K = 4
Q_HEADS = 8
KV_HEADS = 2
ATT_DIM = 64
FF = 2048
TOK_DEV = 256
SEQ_DEV = 1
LENGTH = 1024
SEQS = 2
N_WEIGHT = 2


def shared_keys(key):
    draw = jax.random.truncated_normal(jax.random.fold_in(key, 7), -4.0, 4.0, (D, KV_HEADS, ATT_DIM), jnp.float32)
    return draw * D ** (-0.5)


def draw_keys_values(key, part):
    keys = shared_keys(key)
    vals = jax.random.truncated_normal(jax.random.fold_in(key, 11), -4.0, 4.0, (D, KV_HEADS, ATT_DIM), jnp.float32) * D ** (-0.5)
    return jnp.concatenate([keys, vals], axis=2).reshape(D, KV_HEADS * 2 * ATT_DIM).astype(jnp.bfloat16)


def draw_query_weight(key, part):
    noise = jax.random.truncated_normal(jax.random.fold_in(key, 13), -4.0, 4.0, (D, Q_HEADS, ATT_DIM), jnp.float32) * D ** (-0.5)
    return noise.reshape(D, Q_HEADS * ATT_DIM).astype(jnp.bfloat16)


def levels(key, extent, shards, low, largest):
    factor_of = 1.0
    for axis_at, shards_of in shards:
        heights = jax.random.uniform(jax.random.fold_in(jax.random.fold_in(key, 6), axis_at), (shards_of,), jnp.float32, low / len(shards), largest / len(shards))
        factor_of = factor_of * jnp.repeat(jnp.exp(heights), extent[axis_at] // shards_of).reshape((-1,) + (1,) * (len(extent) - 1 - axis_at))
    return factor_of


def normal_values(stream_key, shape, scale, most, shards=(), kind=jnp.bfloat16):
    level = levels(stream_key, shape, shards, -0.22, 0.18) if shards else 1.0
    array = jax.random.normal(stream_key, shape, jnp.float32) * scale * level
    return jnp.minimum(jnp.maximum(array, -most), most).astype(kind)


def setup_inputs(seed: int = 0) -> dict:
    arg_keys = jax.random.split(jax.random.key(seed), 22)
    layer_input = normal_values(arg_keys[0], (SEQ_DEV, N_WEIGHT * LENGTH, D), 1.0, 6.0, ((1, 8),))
    out_cotangent = normal_values(arg_keys[1], (SEQ_DEV, N_WEIGHT * LENGTH, D), 1.0, 6.0, ((1, 8),))
    input_gain = jnp.clip(1.0 + 0.1 * jax.random.normal(arg_keys[2], (D,), jnp.float32), 0.5, 1.5).astype(jnp.bfloat16)
    mamba_gate = normal_values(arg_keys[3], (D, HEADS * HEAD_DIM), D ** -0.5, 0.1875, ((0, 2), (1, 4)))
    mamba_value = normal_values(arg_keys[4], (D, HEADS * HEAD_DIM), D ** -0.5, 0.1875, ((0, 2), (1, 4)))
    mamba_state = normal_values(arg_keys[5], (D, 2 * STATE), D ** -0.5, 0.1875, ((0, 2),))
    mamba_step = normal_values(arg_keys[6], (D, HEADS), D ** -0.5, 0.1875, ((0, 2), (1, 4)))
    conv_value = normal_values(arg_keys[7], (CONV_K, HEADS * HEAD_DIM), CONV_K ** -0.5, 3.0, ((1, 4),), jnp.float32)
    conv_state = normal_values(arg_keys[8], (CONV_K, 2 * STATE), CONV_K ** -0.5, 3.0, (), jnp.float32)
    step_bias = jnp.clip(-6.5 + 3.5 * jax.random.uniform(arg_keys[9], (HEADS,), jnp.float32) ** levels(arg_keys[9], (HEADS,), ((0, 4),), -0.2, 0.2), -6.5, -3.0)
    decay_log = jnp.clip(-1.0 + 1.7 * jax.random.uniform(arg_keys[10], (HEADS,), jnp.float32) ** levels(arg_keys[10], (HEADS,), ((0, 4),), -0.2, 0.2), -1.0, 0.7)
    skip_gain = jnp.clip(0.5 + 1.0 * jax.random.uniform(arg_keys[11], (HEADS,), jnp.float32) ** levels(arg_keys[11], (HEADS,), ((0, 4),), -0.2, 0.2), 0.5, 1.5)
    mixer_gain = jnp.clip(1.0 + 0.1 * jax.random.normal(arg_keys[12], (HEADS * HEAD_DIM,), jnp.float32), 0.5, 1.5)
    mamba_out = normal_values(arg_keys[13], (HEADS * HEAD_DIM, D), (HEADS * HEAD_DIM) ** -0.5, 0.15625, ((0, 4), (1, 2)))
    query_weight = draw_query_weight(jax.random.fold_in(arg_keys[21], 71), 0)
    keys_values = draw_keys_values(jax.random.fold_in(arg_keys[21], 71), 0)
    attention_out = normal_values(arg_keys[16], (Q_HEADS * ATT_DIM, D), (Q_HEADS * ATT_DIM // 64) ** -0.5, 2.0, ((0, 4), (1, 2)))
    feed_gain = jnp.clip(1.0 + 0.1 * jax.random.normal(arg_keys[17], (D,), jnp.float32), 0.5, 1.5).astype(jnp.bfloat16)
    feed_gate = normal_values(arg_keys[18], (D, FF), D ** -0.5, 0.1875, ((0, 2), (1, 4)))
    feed_up = normal_values(arg_keys[19], (D, FF), D ** -0.5, 0.1875, ((0, 2), (1, 4)))
    feed_down = normal_values(arg_keys[20], (FF, D), FF ** -0.5, 0.125, ((0, 4), (1, 2)))
    return {"layer_input": layer_input, "out_cotangent": out_cotangent, "input_gain": input_gain, "mamba_gate": mamba_gate, "mamba_value": mamba_value, "mamba_state": mamba_state, "mamba_step": mamba_step, "conv_value": conv_value, "conv_state": conv_state, "step_bias": step_bias, "decay_log": decay_log, "skip_gain": skip_gain, "mixer_gain": mixer_gain, "mamba_out": mamba_out, "query_weight": query_weight, "keys_values": keys_values, "attention_out": attention_out, "feed_gain": feed_gain, "feed_gate": feed_gate, "feed_up": feed_up, "feed_down": feed_down}


eps_norm = 1e-05
rope_base = 100000000000.0
highest = lax.Precision.HIGHEST

def to_bf16(vals):
    return lax.optimization_barrier(vals.astype(jnp.bfloat16))

def matmul(left, right):
    return jnp.dot(left, right, preferred_element_type=jnp.float32)

def rms_norm(vals, gain):
    scale = lax.rsqrt(lax.optimization_barrier(jnp.mean(vals * vals, axis=-1, keepdims=True)) + eps_norm)
    return vals * scale * gain

def gated_norm(ssd_out, gate_in, gain):
    count = ssd_out.shape[0]
    heads = gain.shape[0] // HEAD_DIM
    mixed = ssd_out * jax.nn.silu(gate_in)
    grouped = mixed.reshape(count, heads, HEAD_DIM)
    scale = lax.rsqrt(lax.optimization_barrier(jnp.mean(grouped * grouped, axis=-1, keepdims=True)) + eps_norm)
    return (grouped * scale).reshape(count, heads * HEAD_DIM) * gain

def causal_conv(extended, kernel):
    count = extended.shape[0] - kernel.shape[0] + 1
    total = kernel[0] * extended[0:count]
    for tap in range(1, kernel.shape[0]):
        total = total + kernel[tap] * extended[tap:tap + count]
    return jax.nn.silu(total)

def silu_grad(vals):
    sig = jax.nn.sigmoid(vals)
    return sig * (1.0 + vals * (1.0 - sig))

def decay_terms(step_raw, step_bias, decay_log):
    step = jax.nn.softplus(step_raw + step_bias)
    logs = step * -jnp.exp(decay_log)
    return (step, jnp.cumsum(logs, axis=0))

def ssd_block(values, step_raw, step_bias, decay_log, b_mat, c_mat, skip_gain, carried):
    count = values.shape[0]
    heads = step_bias.shape[0]
    step, cum = decay_terms(step_raw, step_bias, decay_log)
    heads_x = values.reshape(count, heads, HEAD_DIM)
    place = jnp.arange(count)
    lower = (place[:, None] >= place[None, :])[:, :, None]
    segment = jnp.where(lower, cum[:, None, :] - cum[None, :, :], -jnp.inf)
    inner = jnp.dot(c_mat, b_mat.T, precision=highest)
    mixing = jnp.exp(segment) * step[None, :, :] * inner[:, :, None]
    out = jnp.einsum('tsh,shp->thp', mixing, heads_x, precision=highest)
    out = out + jnp.exp(cum)[:, :, None] * jnp.einsum('hpn,tn->thp', carried, c_mat, precision=highest)
    out = out + skip_gain[None, :, None] * heads_x
    weight_tail = jnp.exp(cum[-1][None, :] - cum) * step
    local_state = jnp.einsum('sh,shp,sn->hpn', weight_tail, heads_x, b_mat, precision=highest)
    end_state = jnp.exp(cum[-1])[:, None, None] * carried + local_state
    return (out.reshape(count, heads * HEAD_DIM), end_state)

def ssd_sequence(values, step_raw, step_bias, decay_log, b_mat, c_mat, skip_gain):
    blocks = values.shape[0] // TOK_DEV
    pieces = (values.reshape(blocks, TOK_DEV, -1), step_raw.reshape(blocks, TOK_DEV, -1), b_mat.reshape(blocks, TOK_DEV, -1), c_mat.reshape(blocks, TOK_DEV, -1))

    def advance(carried, piece):
        out, end_state = ssd_block(piece[0], piece[1], step_bias, decay_log, piece[2], piece[3], skip_gain, carried)
        return (end_state, out)
    start = jnp.zeros((step_bias.shape[0], HEAD_DIM, STATE), jnp.float32)
    _, outs = lax.scan(advance, start, pieces)
    return outs.reshape(values.shape[0], -1)

def rope_tables(first_row, count):
    half = ATT_DIM // 2
    freqs = rope_base ** (-(2.0 * jnp.arange(half).astype(jnp.float32)) / ATT_DIM)
    angles = (first_row + jnp.arange(count)).astype(jnp.float32)[:, None] * freqs[None, :]
    return (jnp.cos(angles), jnp.sin(angles))

def rotate(vals, cosines, sines):
    count = vals.shape[0]
    grouped = vals.reshape(count, -1, ATT_DIM)
    half = ATT_DIM // 2
    first = grouped[:, :, :half]
    second = grouped[:, :, half:]
    cos_three = cosines[:, None, :]
    sin_three = sines[:, None, :]
    out = jnp.concatenate([first * cos_three - second * sin_three, second * cos_three + first * sin_three], axis=2)
    return out.reshape(count, -1)

def layer_sequence(layer_in, cotangent, params):
    input_gain, mamba_gate, mamba_value, mamba_state, mamba_step, conv_value, conv_state, step_bias, decay_log, skip_gain, mixer_gain, mamba_out, query_weight, keys_values, attention_out, feed_gain, feed_gate, feed_up, feed_down = params
    length = layer_in.shape[0]
    width = HEADS * HEAD_DIM
    group = Q_HEADS // KV_HEADS
    scale = ATT_DIM ** (-0.5)
    inputs = layer_in.astype(jnp.float32)
    normed_f, norm_one_vjp = jax.vjp(rms_norm, inputs, input_gain.astype(jnp.float32))
    normed = to_bf16(normed_f)
    gate_lin = matmul(normed, mamba_gate)
    value_lin = matmul(normed, mamba_value)
    state_lin = matmul(normed, mamba_state)
    step_raw = matmul(normed, mamba_step)
    kernel = jnp.concatenate([conv_value, conv_state], axis=1)
    pre = jnp.concatenate([value_lin, state_lin], axis=1)
    extended = jnp.concatenate([jnp.zeros((CONV_K - 1, pre.shape[1]), jnp.float32), pre], axis=0)
    activated, conv_vjp = jax.vjp(causal_conv, extended, kernel)
    values = activated[:, :width]
    b_mat = activated[:, width:width + STATE]
    c_mat = activated[:, width + STATE:]
    ssd_out, ssd_vjp = jax.vjp(ssd_sequence, values, step_raw, step_bias, decay_log, b_mat, c_mat, skip_gain)
    gated, gate_vjp = jax.vjp(gated_norm, ssd_out, gate_lin, mixer_gain)
    mixer_in = to_bf16(gated)
    cosines, sines = rope_tables(0, length)
    queries = to_bf16(rotate(matmul(normed, query_weight), cosines, sines))
    pair_raw = matmul(normed, keys_values).reshape(length, KV_HEADS, 2 * ATT_DIM)
    keys_rot = rotate(pair_raw[:, :, :ATT_DIM].reshape(length, -1), cosines, sines).reshape(length, KV_HEADS, ATT_DIM)
    pairs = to_bf16(jnp.concatenate([keys_rot, pair_raw[:, :, ATT_DIM:]], axis=2))
    query_three = queries.astype(jnp.float32).reshape(length, Q_HEADS, ATT_DIM)
    keys_full = jnp.repeat(pairs[:, :, :ATT_DIM].astype(jnp.float32), group, axis=1)
    vals_full = jnp.repeat(pairs[:, :, ATT_DIM:].astype(jnp.float32), group, axis=1)
    place = jnp.arange(length)
    visible = place[None, :] <= place[:, None]
    scores = jnp.where(visible[None], jnp.einsum('qhd,khd->hqk', query_three, keys_full) * scale, -jnp.inf)
    peak = lax.optimization_barrier(jnp.max(scores, axis=2, keepdims=True))
    expo = jnp.exp(scores - peak)
    total = lax.optimization_barrier(jnp.sum(expo, axis=2, keepdims=True))
    logsum = peak + jnp.log(total)
    probs = to_bf16(expo / total).astype(jnp.float32)
    attended = to_bf16(jnp.einsum('hqk,khd->qhd', probs, vals_full).reshape(length, -1))
    hidden_in = inputs + matmul(mixer_in, mamba_out) + matmul(attended, attention_out)
    normed_two_f, norm_two_vjp = jax.vjp(rms_norm, hidden_in, feed_gain.astype(jnp.float32))
    normed_two = to_bf16(normed_two_f)
    gate_ff = matmul(normed_two, feed_gate)
    up_ff = matmul(normed_two, feed_up)
    hidden = to_bf16(jax.nn.silu(gate_ff) * up_ff)
    layer_out = (hidden_in + matmul(hidden, feed_down)).astype(jnp.bfloat16)
    grad_hidden = matmul(cotangent, feed_down.T)
    feed_down_grad = matmul(hidden.T, cotangent)
    gate_ff_grad = to_bf16(grad_hidden * up_ff * silu_grad(gate_ff))
    up_ff_grad = to_bf16(grad_hidden * jax.nn.silu(gate_ff))
    feed_gate_grad = matmul(normed_two.T, gate_ff_grad)
    feed_up_grad = matmul(normed_two.T, up_ff_grad)
    grad_two = matmul(gate_ff_grad, feed_gate.T) + matmul(up_ff_grad, feed_up.T)
    grad_res, feed_gain_grad = norm_two_vjp(grad_two)
    grad_hidden_in = cotangent.astype(jnp.float32) + grad_res
    grad_mix = to_bf16(grad_hidden_in)
    mamba_out_grad = matmul(mixer_in.T, grad_mix)
    attention_out_grad = matmul(attended.T, grad_mix)
    grad_mixer = matmul(grad_mix, mamba_out.T)
    grad_att = to_bf16(matmul(grad_mix, attention_out.T))
    grad_heads = grad_att.astype(jnp.float32).reshape(length, Q_HEADS, ATT_DIM)
    probs_f = jnp.exp(scores - logsum)
    grad_probs = jnp.einsum('qhd,khd->hqk', grad_heads, vals_full)
    delta = lax.optimization_barrier(jnp.sum(probs_f * grad_probs, axis=2, keepdims=True))
    grad_scores = to_bf16(probs_f * (grad_probs - delta)).astype(jnp.float32)
    grad_query = jnp.einsum('hqk,khd->qhd', grad_scores, keys_full).reshape(length, -1) * scale
    grad_keys = jnp.einsum('hqk,qhd->khd', grad_scores, query_three) * scale
    grad_keys = lax.optimization_barrier(jnp.sum(grad_keys.reshape(length, KV_HEADS, group, ATT_DIM), axis=2))
    grad_vals = jnp.einsum('hqk,qhd->khd', to_bf16(probs_f).astype(jnp.float32), grad_heads)
    grad_vals = lax.optimization_barrier(jnp.sum(grad_vals.reshape(length, KV_HEADS, group, ATT_DIM), axis=2))
    query_lb = to_bf16(rotate(grad_query, cosines, -sines))
    keys_back = rotate(grad_keys.reshape(length, -1), cosines, -sines).reshape(length, KV_HEADS, ATT_DIM)
    pair_lb = to_bf16(jnp.concatenate([keys_back, grad_vals], axis=2).reshape(length, -1))
    grad_ssd, grad_gate_lin, mixer_gain_grad = gate_vjp(grad_mixer)
    grad_values, grad_step_raw, step_bias_grad, decay_log_grad, grad_b, grad_c, skip_gain_grad = ssd_vjp(grad_ssd)
    grad_ext, kernel_grad = conv_vjp(jnp.concatenate([grad_values, grad_b, grad_c], axis=1))
    grad_pre = grad_ext[CONV_K - 1:]
    gate_lb = to_bf16(grad_gate_lin)
    value_lb = to_bf16(grad_pre[:, :width])
    state_lb = to_bf16(grad_pre[:, width:])
    step_lb = to_bf16(grad_step_raw)
    grad_normed = matmul(gate_lb, mamba_gate.T) + matmul(value_lb, mamba_value.T) + matmul(state_lb, mamba_state.T) + matmul(step_lb, mamba_step.T) + matmul(query_lb, query_weight.T) + matmul(pair_lb, keys_values.T)
    grad_res_one, input_gain_grad = norm_one_vjp(grad_normed)
    input_grad = grad_hidden_in + grad_res_one
    grads = (input_gain_grad, matmul(normed.T, gate_lb), matmul(normed.T, value_lb), matmul(normed.T, state_lb), matmul(normed.T, step_lb), kernel_grad[:, :width], kernel_grad[:, width:], step_bias_grad, decay_log_grad, skip_gain_grad, mixer_gain_grad, mamba_out_grad, matmul(normed.T, query_lb), matmul(normed.T, pair_lb), attention_out_grad, feed_gain_grad, feed_gate_grad, feed_up_grad, feed_down_grad)
    return (layer_out, input_grad, grads)

def reference(layer_input, out_cotangent, input_gain, mamba_gate, mamba_value, mamba_state, mamba_step, conv_value, conv_state, step_bias, decay_log, skip_gain, mixer_gain, mamba_out, query_weight, keys_values, attention_out, feed_gain, feed_gate, feed_up, feed_down):
    params = (input_gain, mamba_gate, mamba_value, mamba_state, mamba_step, conv_value, conv_state, step_bias, decay_log, skip_gain, mixer_gain, mamba_out, query_weight, keys_values, attention_out, feed_gain, feed_gate, feed_up, feed_down)
    shaped_in = layer_input.reshape(SEQS, LENGTH, D)
    shaped_cot = out_cotangent.reshape(SEQS, LENGTH, D)
    start = tuple((jnp.zeros(param.shape, jnp.float32) for param in params))

    def advance(totals, pieces):
        out, grad_in, grads = layer_sequence(pieces[0], pieces[1], params)
        return (tuple((left + right for left, right in zip(totals, grads))), (out, grad_in))
    totals, (outs, grads_in) = lax.scan(advance, start, (shaped_in, shaped_cot))
    return (outs.reshape(SEQ_DEV, N_WEIGHT * LENGTH, D), grads_in.reshape(SEQ_DEV, N_WEIGHT * LENGTH, D), totals[0], totals[1], totals[2], totals[3], totals[4], totals[5], totals[6], totals[7], totals[8], totals[9], totals[10], totals[11], totals[12], totals[13], totals[14], totals[15], totals[16], totals[17], totals[18])
```

```python
import jax
import jax.numpy as jnp
from jax import lax
from jax.sharding import PartitionSpec as P

HEAD_DIM = 64
STATE = 128
Q_HEADS = 8
KV_HEADS = 2
ATT_DIM = 64


eps_norm = 1e-05
rope_base = 100000000000.0
highest = lax.Precision.HIGHEST


def passed_along(value, axis, steps):
    count = lax.axis_size(axis)
    initial, last = (max(0, -steps), min(count, count - steps))
    return lax.ppermute(value, axis, [(source, source + steps) for source in range(initial, last)])


def entering(value, axis, join, neutral, backward):
    count, mine = (lax.axis_size(axis), lax.axis_index(axis))
    pieces = jax.tree.map(lambda part: lax.all_gather(part, axis), value)
    if backward:
        pieces = jax.tree.map(lambda part: part[::-1], pieces)
        mine = count - 1 - mine
    so_far = jax.tree.map(
        lambda part, zero: jnp.full_like(part, 0) + jnp.asarray(zero, part.dtype), value, neutral
    )

    def step(position, so_far):
        longer = join(so_far, jax.tree.map(lambda part: part[position], pieces))
        return jax.tree.map(lambda new, old: jnp.where(position < mine, new, old), longer, so_far)

    return lax.fori_loop(0, count - 1, step, so_far)


def as_sent(array):
    return jax.tree.map(lambda a: a.astype(jnp.bfloat16) if a.dtype == jnp.float32 else a, array)


def matmul(left, right):
    return jnp.dot(left, right, preferred_element_type=jnp.float32)


def rms_norm(vals, gain):
    scale = lax.rsqrt(jnp.mean(vals * vals, axis=-1, keepdims=True) + eps_norm)
    return vals * scale * gain


def gated_norm(ssd_out, gate_in, gain):
    count = ssd_out.shape[0]
    heads = gain.shape[0] // HEAD_DIM
    mixed = ssd_out * jax.nn.silu(gate_in)
    grouped = mixed.reshape(count, heads, HEAD_DIM)
    scale = lax.rsqrt(jnp.mean(grouped * grouped, axis=-1, keepdims=True) + eps_norm)
    return (grouped * scale).reshape(count, heads * HEAD_DIM) * gain


def causal_conv(extended, kernel):
    count = extended.shape[0] - kernel.shape[0] + 1
    total = kernel[0] * extended[0:count]
    for tap in range(1, kernel.shape[0]):
        total = total + kernel[tap] * extended[tap : tap + count]
    return jax.nn.silu(total)


def silu_grad(vals):
    sig = jax.nn.sigmoid(vals)
    return sig * (1.0 + vals * (1.0 - sig))


def decay_terms(step_raw, step_bias, decay_log):
    step = jax.nn.softplus(step_raw + step_bias)
    logs = step * -jnp.exp(decay_log)
    return (step, jnp.cumsum(logs, axis=0))


def ssd_block(values, step_raw, step_bias, decay_log, b_mat, c_mat, skip_gain, carried):
    count = values.shape[0]
    heads = step_bias.shape[0]
    step, cum = decay_terms(step_raw, step_bias, decay_log)
    heads_x = values.reshape(count, heads, HEAD_DIM)
    place = jnp.arange(count)
    lower = (place[:, None] >= place[None, :])[:, :, None]
    segment = jnp.where(lower, cum[:, None, :] - cum[None, :, :], -jnp.inf)
    inner = jnp.dot(c_mat, b_mat.T, precision=highest)
    mixing = jnp.exp(segment) * step[None, :, :] * inner[:, :, None]
    out = jnp.einsum("tsh,shp->thp", mixing, heads_x, precision=highest)
    out = out + jnp.exp(cum)[:, :, None] * jnp.einsum(
        "hpn,tn->thp", carried, c_mat, precision=highest
    )
    out = out + skip_gain[None, :, None] * heads_x
    weight_tail = jnp.exp(cum[-1][None, :] - cum) * step
    local_state = jnp.einsum("sh,shp,sn->hpn", weight_tail, heads_x, b_mat, precision=highest)
    end_state = jnp.exp(cum[-1])[:, None, None] * carried + local_state
    return (out.reshape(count, heads * HEAD_DIM), end_state)


def carried_term(cum, c_mat, carried):
    count = c_mat.shape[0]
    term = jnp.exp(cum)[:, :, None] * jnp.einsum("hpn,tn->thp", carried, c_mat, precision=highest)
    return term.reshape(count, -1)


def combine_states(earlier, later):
    return (earlier[0] * later[0], later[0][..., None, None] * earlier[1] + later[1])


def rope_tables(first_row, count):
    half = ATT_DIM // 2
    freqs = rope_base ** (-(2.0 * jnp.arange(half).astype(jnp.float32)) / ATT_DIM)
    angles = (first_row + jnp.arange(count)).astype(jnp.float32)[:, None] * freqs[None, :]
    return (jnp.cos(angles), jnp.sin(angles))


def rotate(vals, cosines, sines):
    count = vals.shape[0]
    grouped = vals.reshape(count, -1, ATT_DIM)
    half = ATT_DIM // 2
    first = grouped[:, :, :half]
    second = grouped[:, :, half:]
    cos_three = cosines[:, None, :]
    sin_three = sines[:, None, :]
    out = jnp.concatenate(
        [first * cos_three - second * sin_three, second * cos_three + first * sin_three], axis=2
    )
    return out.reshape(count, -1)


def attention_scores(queries, pairs, first_row):
    count = queries.shape[0]
    grouped = queries.reshape(count, -1, ATT_DIM)
    scores = jnp.einsum(
        "qhd,kd->hqk", grouped, pairs[:, :ATT_DIM], preferred_element_type=jnp.float32
    ) * ATT_DIM ** (-0.5)
    visible = jnp.arange(pairs.shape[0])[None, :] <= (first_row + jnp.arange(count))[:, None]
    return jnp.where(visible[None], scores, -jnp.inf)


bf16 = jnp.bfloat16
f32 = jnp.float32


def swapped(value, axis, bit):
    count = lax.axis_size(axis)
    return lax.ppermute(value, axis, [(i, i ^ bit) for i in range(count)])


def shifted(value, axis, steps):
    count = lax.axis_size(axis)
    return lax.ppermute(value, axis, [(i, (i + steps) % count) for i in range(count)])


def bits_of(count):
    bits = []
    bit = count // 2
    while bit:
        bits.append(bit)
        bit //= 2
    return bits


def block_masks(count):
    masks = [0]
    for bit in bits_of(count):
        masks = masks + [mask ^ bit for mask in masks]
    return masks


def collect_blocks(value, axis):
    held = value[None]
    for bit in bits_of(lax.axis_size(axis)):
        held = jnp.concatenate([held, swapped(held, axis, bit)], axis=0)
    return held


def scatter_blocks(held, axis, sent):
    for bit in reversed(bits_of(lax.axis_size(axis))):
        half = held.shape[0] // 2
        got = swapped(held[half:].astype(sent), axis, bit)
        held = held[:half].astype(f32) + got.astype(f32)
    return held[0]


def pick(low, high, index):
    return jnp.where(index == 0, jnp.concatenate([low, high]), jnp.concatenate([high, low]))


def paired():
    return lax.axis_size("weight") == 2 and lax.axis_size("context") % 2 == 0


def gather_first(pack):
    if not paired():
        return lax.all_gather(pack, "weight", axis=0, tiled=True)
    core = lax.axis_index("context") % 2
    half = pack.shape[0] // 2
    got = swapped(lax.dynamic_slice_in_dim(pack, core * half, half), "weight", 1)
    other = swapped(got, "context", 1)
    return pick(pack, pick(got, other, core), lax.axis_index("weight"))


def reduce_first(grad):
    if not paired():
        part = lax.psum_scatter(grad.astype(bf16), "weight", scatter_dimension=0, tiled=True)
        return lax.psum(part, "context").astype(f32)
    core = lax.axis_index("context") % 2
    mine = lax.axis_index("weight")
    four = grad.reshape(2, 2, grad.shape[0] // 4, grad.shape[1])
    got = swapped(lax.dynamic_slice_in_dim(four, 1 - core, 1, 1).astype(bf16), "context", 1)
    held = lax.dynamic_slice_in_dim(four, core, 1, 1)[:, 0] + got[:, 0].astype(f32)
    got = swapped(lax.dynamic_slice_in_dim(held, 1 - mine, 1, 0).astype(bf16), "weight", 1)
    held = (lax.dynamic_slice_in_dim(held, mine, 1, 0) + got.astype(f32))[0]
    bit = lax.axis_size("context") // 2
    while bit > 1:
        sent = held.astype(bf16)
        held = sent.astype(f32) + swapped(sent, "context", bit).astype(f32)
        bit //= 2
    held = held.astype(bf16)
    return pick(held, swapped(held, "context", 1), core).astype(f32)


def sum_small(value):
    bit = lax.axis_size("context") // 2
    while bit:
        value = value + swapped(value, "context", bit)
        bit //= 2
    if lax.axis_size("weight") == 2:
        return value + swapped(value, "weight", 1)
    return lax.psum(value, "weight")


def sum_heads(value):
    for bit in bits_of(lax.axis_size("tensor")):
        value = value + swapped(value, "tensor", bit)
    return value


def rotated_rows(value, rank):
    count = lax.axis_size("tensor")
    rows = value.shape[0] // count
    return [
        lax.dynamic_slice_in_dim(value, ((rank - s) % count) * rows, rows) for s in range(count)
    ]


def head_scatter(blocks):
    count = lax.axis_size("tensor")
    total = blocks[0].astype(f32)
    got = [shifted(blocks[s].astype(bf16), "tensor", -s) for s in range(1, count)]
    for part in got:
        total = total + part.astype(f32)
    return total


def head_blocks(value):
    count = lax.axis_size("tensor")
    return [value] + [shifted(value, "tensor", s) for s in range(1, count)]


def in_order(blocks, rank, axis):
    count = len(blocks)
    whole = jnp.concatenate(blocks[::-1] + blocks[:0:-1], axis=axis)
    size = blocks[0].shape[axis]
    return lax.dynamic_slice_in_dim(whole, (count - 1 - rank) * size, size * count, axis)


def local(
    layer_input,
    out_cotangent,
    input_gain,
    mamba_gate,
    mamba_value,
    mamba_state,
    mamba_step,
    conv_value,
    conv_state,
    step_bias,
    decay_log,
    skip_gain,
    mixer_gain,
    mamba_out,
    query_weight,
    keys_values,
    attention_out,
    feed_gain,
    feed_gate,
    feed_up,
    feed_down,
):
    count = layer_input.shape[1]
    width = layer_input.shape[2]
    ranks = lax.axis_size("tensor")
    blocks = lax.axis_size("context")
    block = lax.axis_index("context")
    rank = lax.axis_index("tensor")
    first_row = block * count
    slice_rows = count // ranks
    heads = step_bias.shape[0]
    inner = heads * HEAD_DIM
    pad_step = -heads % 128
    rows_in = layer_input.reshape(count, width)
    cotangent = out_cotangent.reshape(count, width)

    gains = jnp.stack([input_gain, feed_gain])
    gains = gains[:, None, :]
    if lax.axis_size("weight") == 2:
        other = swapped(gains, "weight", 1)
        mine = lax.axis_index("weight")
        gains = jnp.where(
            mine == 0,
            jnp.concatenate([gains, other], axis=1),
            jnp.concatenate([other, gains], axis=1),
        )
    else:
        gains = lax.all_gather(gains, "weight", axis=1, tiled=True)
    gains = gains.reshape(2, width).astype(f32)
    norm_one, norm_two = gains[0], gains[1]

    step_pad = jnp.pad(mamba_step, ((0, 0), (0, pad_step)))
    first_pack = gather_first(jnp.concatenate([mamba_value, mamba_state, step_pad], axis=1))
    second_pack = gather_first(jnp.concatenate([keys_values, query_weight, mamba_gate], axis=1))
    out_pack = gather_first(jnp.concatenate([mamba_out, attention_out], axis=0).T)
    feed_pack = gather_first(jnp.concatenate([feed_gate, feed_up, feed_down.T], axis=1))

    pair_cols = keys_values.shape[1]
    att_cols = query_weight.shape[1]
    pair_full = second_pack[:, :pair_cols]
    query_full = second_pack[:, pair_cols : pair_cols + att_cols]
    gate_full = second_pack[:, pair_cols + att_cols :]
    state_cols = mamba_state.shape[1]
    state_full = first_pack[:, inner : inner + state_cols]
    ff_local = feed_gate.shape[1]

    inputs = rows_in.astype(f32)
    normed_f, norm_one_vjp = jax.vjp(rms_norm, inputs, norm_one)
    normed = normed_f.astype(bf16)
    lin = matmul(normed, first_pack)
    pre = lin[:, : inner + state_cols]
    step_raw = lin[:, inner + state_cols : inner + state_cols + heads]
    kernel = jnp.concatenate([conv_value, conv_state], axis=1)
    taps = kernel.shape[0]
    edge = count - taps + 1
    tail = passed_along(pre[edge:], "context", 1)
    lin_two = matmul(normed, second_pack)
    gate_lin = lin_two[:, pair_cols + att_cols :]
    query_raw = lin_two[:, pair_cols : pair_cols + att_cols]
    local_heads = att_cols // ATT_DIM
    head_group = rank * local_heads // (Q_HEADS // KV_HEADS)
    pair_raw = lax.dynamic_slice_in_dim(lin_two[:, :pair_cols], head_group * 2 * ATT_DIM, 2 * ATT_DIM, 1)
    cosines, sines = rope_tables(first_row, count)
    queries = rotate(query_raw, cosines, sines).astype(bf16)
    pair_rot = jnp.concatenate(
        [rotate(pair_raw[:, :ATT_DIM], cosines, sines), pair_raw[:, ATT_DIM:]], axis=1
    ).astype(bf16)
    all_pairs = collect_blocks(pair_rot, "context").reshape(blocks * count, 2 * ATT_DIM)

    extended = jnp.concatenate([tail, pre], axis=0)
    activated, conv_vjp = jax.vjp(causal_conv, extended, kernel)
    values = activated[:, :inner]
    b_mat = activated[:, inner : inner + STATE]
    c_mat = activated[:, inner + STATE :]
    empty_state = jnp.zeros((heads, HEAD_DIM, STATE), f32)
    intra, local_state = ssd_block(
        values, step_raw, step_bias, decay_log, b_mat, c_mat, skip_gain, empty_state
    )
    _, cum = decay_terms(step_raw, step_bias, decay_log)
    decay_total = jnp.exp(cum[-1])
    masks = block_masks(blocks)
    decay_row = jnp.pad(decay_total, (0, STATE - heads))[None]
    decay_rows = jnp.pad(decay_row, ((0, 7), (0, 0)))
    packed = jnp.concatenate([local_state.reshape(heads * HEAD_DIM, STATE), decay_rows], axis=0)
    held = collect_blocks(packed, "context")
    held_decay = held[:, heads * HEAD_DIM, :heads]
    held_state = held[:, : heads * HEAD_DIM].reshape(blocks, heads, HEAD_DIM, STATE)
    places = jnp.stack([block ^ mask for mask in masks])

    def entering_state(states, backward):
        ahead = (lambda a, b: a > b) if backward else (lambda a, b: a < b)
        total = jnp.zeros_like(states[0])
        for at in range(1, blocks):
            weight = jnp.ones((heads,), f32)
            for mid in range(1, blocks):
                between = ahead(places[at], places[mid]) & ahead(places[mid], block)
                weight = weight * jnp.where(between, held_decay[mid], 1.0)
            weight = jnp.where(ahead(places[at], block), weight, 0.0)
            total = total + weight[:, None, None] * states[at]
        return total

    carried = entering_state(held_state, False)
    ssd_out = intra + carried_term(cum, c_mat, carried)
    gated, gate_vjp = jax.vjp(gated_norm, ssd_out, gate_lin, mixer_gain)
    mixer_in = gated.astype(bf16)

    query_three = queries.reshape(count, local_heads, ATT_DIM)
    key_place = (places[:, None] * count + jnp.arange(count)[None]).reshape(-1)
    visible = key_place[None, :] <= (first_row + jnp.arange(count))[:, None]
    scores = jnp.einsum(
        "qhd,kd->hqk", query_three, all_pairs[:, :ATT_DIM], preferred_element_type=f32
    ) * ATT_DIM ** (-0.5)
    scores = jnp.where(visible[None], scores, -jnp.inf)
    peak = jnp.max(scores, axis=2, keepdims=True)
    expo = jnp.exp(scores - peak)
    total = jnp.sum(expo, axis=2, keepdims=True)
    logsum = peak + jnp.log(total)
    probs = (expo / total).astype(bf16)
    attended = jnp.einsum(
        "hqk,kd->qhd", probs, all_pairs[:, ATT_DIM:], preferred_element_type=f32
    )
    attend_in = attended.reshape(count, -1).astype(bf16)
    mix_in = jnp.concatenate([mixer_in, attend_in], axis=1)
    mixed = lax.dot_general(mix_in, out_pack, (((1,), (1,)), ((), ())), preferred_element_type=f32)
    mixed = head_scatter(rotated_rows(mixed, rank))
    hidden_in = lax.dynamic_slice_in_dim(inputs, rank * slice_rows, slice_rows) + mixed
    normed_two_f, norm_two_vjp = jax.vjp(rms_norm, hidden_in, norm_two)
    normed_two = jnp.concatenate(head_blocks(normed_two_f.astype(bf16)), axis=0)

    cot_rot = jnp.concatenate(rotated_rows(cotangent, rank), axis=0)
    ff = matmul(normed_two, feed_pack[:, : 2 * ff_local])
    gate_ff = ff[:, :ff_local]
    up_ff = ff[:, ff_local:]
    silu_ff = jax.nn.silu(gate_ff)
    hidden = (silu_ff * up_ff).astype(bf16)
    down_t = feed_pack[:, 2 * ff_local :]
    grad_hidden = matmul(cot_rot, down_t)
    gate_ff_grad = (grad_hidden * up_ff * silu_grad(gate_ff)).astype(bf16)
    up_ff_grad = (grad_hidden * silu_ff).astype(bf16)
    both_ff = jnp.concatenate([gate_ff_grad, up_ff_grad], axis=1)
    grad_two = lax.dot_general(
        both_ff, feed_pack[:, : 2 * ff_local], (((1,), (1,)), ((), ())), preferred_element_type=f32
    )
    grad_two = head_scatter(jnp.split(grad_two, ranks))
    down_out = lax.dot_general(hidden, down_t, (((1,), (1,)), ((), ())), preferred_element_type=f32)
    down_out = head_scatter(jnp.split(down_out, ranks))
    layer_output = (hidden_in + down_out).astype(bf16)
    layer_output = in_order(head_blocks(layer_output), rank, 0)[None]

    feed_grad = jnp.concatenate(
        [matmul(normed_two.T, both_ff), matmul(cot_rot.T, hidden)], axis=1
    )
    feed_reduced = reduce_first(feed_grad)

    grad_res, feed_gain_grad = norm_two_vjp(grad_two)
    cot_slice = lax.dynamic_slice_in_dim(cotangent, rank * slice_rows, slice_rows).astype(f32)
    grad_hidden_in = cot_slice + grad_res
    grad_mix = in_order(head_blocks(grad_hidden_in.astype(bf16)), rank, 0)
    out_reduced = reduce_first(matmul(grad_mix.T, mix_in))
    back = matmul(grad_mix, out_pack)
    grad_mixer = back[:, :inner]
    grad_heads = back[:, inner:].astype(bf16).reshape(count, local_heads, ATT_DIM)

    grad_ssd, grad_gate_lin, mixer_gain_grad = gate_vjp(grad_mixer)
    gate_lb = grad_gate_lin.astype(bf16)
    grad_three = grad_ssd.reshape(count, heads, HEAD_DIM)
    summary = jnp.einsum("th,thp,tn->hpn", jnp.exp(cum), grad_three, c_mat, precision=highest)
    held_later = collect_blocks(summary, "context")
    later = entering_state(held_later, True)

    probs_f = jnp.exp(scores - logsum)
    grad_probs = jnp.einsum(
        "qhd,kd->hqk", grad_heads, all_pairs[:, ATT_DIM:], preferred_element_type=f32
    )
    delta = jnp.sum(probs_f * grad_probs, axis=2, keepdims=True)
    grad_scores = (probs_f * (grad_probs - delta)).astype(bf16)
    scale = ATT_DIM ** (-0.5)
    grad_query = (
        jnp.einsum("hqk,kd->qhd", grad_scores, all_pairs[:, :ATT_DIM], preferred_element_type=f32)
        * scale
    ).reshape(count, -1)
    grad_keys = jnp.einsum("hqk,qhd->kd", grad_scores, query_three, preferred_element_type=f32) * scale
    grad_vals = jnp.einsum("hqk,qhd->kd", probs_f.astype(bf16), grad_heads, preferred_element_type=f32)
    pair_grad = jnp.concatenate([grad_keys, grad_vals], axis=1).reshape(blocks, count, 2 * ATT_DIM)
    own_pair = scatter_blocks(pair_grad, "context", bf16)
    query_lb = rotate(grad_query, cosines, -sines).astype(bf16)
    pair_back = jnp.concatenate(
        [rotate(own_pair[:, :ATT_DIM], cosines, -sines), own_pair[:, ATT_DIM:]], axis=1
    )
    placed = in_order(head_blocks(pair_back.astype(bf16)), rank, 1)
    placed = placed.reshape(count, KV_HEADS, ranks // KV_HEADS, 2 * ATT_DIM).astype(f32)
    pair_lb = jnp.sum(placed, axis=2).reshape(count, pair_cols).astype(bf16)

    def ssd_local(local_values, local_raw, local_bias, local_decay, local_b, local_c, local_skip):
        return ssd_block(
            local_values, local_raw, local_bias, local_decay, local_b, local_c, local_skip, carried
        )

    _, ssd_vjp = jax.vjp(ssd_local, values, step_raw, step_bias, decay_log, b_mat, c_mat, skip_gain)
    grad_values, grad_step_raw, step_bias_grad, decay_log_grad, grad_b, grad_c, skip_gain_grad = (
        ssd_vjp((grad_ssd, later))
    )
    cols = state_cols // ranks
    grad_bc = jnp.concatenate([grad_b, grad_c], axis=1)
    bc_blocks = [
        lax.dynamic_slice_in_dim(grad_bc, ((rank - s) % ranks) * cols, cols, 1) for s in range(ranks)
    ]
    grad_bc = head_scatter(bc_blocks)

    def sliced(array):
        state_part = lax.dynamic_slice_in_dim(array, inner + rank * cols, cols, array.ndim - 1)
        return jnp.concatenate([array[..., :inner], state_part], axis=-1)

    _, conv_back = jax.vjp(causal_conv, sliced(extended), sliced(kernel))
    grad_ext, kernel_grad = conv_back(jnp.concatenate([grad_values, grad_bc], axis=1))
    spill = passed_along(grad_ext[: taps - 1], "context", -1)
    grad_pre = jnp.concatenate(
        [grad_ext[taps - 1 : taps - 1 + edge], grad_ext[taps - 1 + edge :] + spill], axis=0
    )
    value_lb = grad_pre[:, :inner].astype(bf16)
    state_part = grad_pre[:, inner:].astype(bf16)
    state_lb = in_order(head_blocks(state_part), rank, 1)
    step_lb = jnp.pad(grad_step_raw.astype(bf16), ((0, 0), (0, pad_step)))
    pcols = pair_cols // ranks
    pair_part = lax.dynamic_slice_in_dim(pair_lb, rank * pcols, pcols, 1)
    pair_weight = lax.dynamic_slice_in_dim(pair_full, rank * pcols, pcols, 1)
    state_weight = lax.dynamic_slice_in_dim(state_full, rank * cols, cols, 1)
    lbs = jnp.concatenate([value_lb, step_lb, query_lb, gate_lb, state_part, pair_part], axis=1)
    weights = jnp.concatenate(
        [
            first_pack[:, :inner],
            first_pack[:, inner + state_cols :],
            query_full,
            gate_full,
            state_weight,
            pair_weight,
        ],
        axis=1,
    )
    part = lax.dot_general(lbs, weights, (((1,), (1,)), ((), ())), preferred_element_type=f32)
    grad_normed = head_scatter(rotated_rows(part, rank))
    input_slice = lax.dynamic_slice_in_dim(inputs, rank * slice_rows, slice_rows)
    _, norm_slice_vjp = jax.vjp(rms_norm, input_slice, norm_one)
    grad_res_one, gain_one_grad = norm_slice_vjp(grad_normed)
    input_grad = in_order(
        head_blocks((grad_hidden_in + grad_res_one).astype(bf16)), rank, 0
    ).astype(f32)[None]

    early = reduce_first(matmul(normed.T, jnp.concatenate([gate_lb, query_lb, pair_lb], axis=1)))
    late = reduce_first(matmul(normed.T, jnp.concatenate([value_lb, step_lb, state_lb], axis=1)))

    flat = jnp.concatenate(
        [
            kernel_grad[:, :inner].reshape(-1),
            mixer_gain_grad,
            step_bias_grad,
            decay_log_grad,
            skip_gain_grad,
        ]
    )
    own_size = flat.shape[0]
    state_kernel = lax.dynamic_update_slice(
        jnp.zeros((taps, state_cols), f32), kernel_grad[:, inner:], (jnp.int32(0), rank * cols)
    )
    shared = jnp.concatenate([gain_one_grad, feed_gain_grad, state_kernel.reshape(-1)])
    shared_size = shared.shape[0]
    small = jnp.concatenate([shared, flat])
    small = jnp.pad(small, (0, -small.shape[0] % 1024)).reshape(-1, 128)
    small = sum_small(small).reshape(-1)
    flat = small[shared_size : shared_size + own_size]
    shared = small[:shared_size]
    shared = jnp.pad(shared, (0, -shared_size % 1024)).reshape(-1, 128)
    shared = sum_heads(shared).reshape(-1)
    part_rows = width // lax.axis_size("weight")
    mine = lax.axis_index("weight") * part_rows
    ends = [taps * inner, taps * inner + inner]
    ends = ends + [ends[-1] + heads, ends[-1] + 2 * heads, ends[-1] + 3 * heads]
    return (
        layer_output,
        input_grad,
        lax.dynamic_slice_in_dim(shared[:width], mine, part_rows),
        early[:, :inner],
        late[:, :inner],
        late[:, inner + heads + pad_step :],
        late[:, inner : inner + heads],
        flat[: ends[0]].reshape(taps, inner),
        shared[2 * width : 2 * width + taps * state_cols].reshape(taps, state_cols),
        flat[ends[1] : ends[2]],
        flat[ends[2] : ends[3]],
        flat[ends[3] : ends[4]],
        flat[ends[0] : ends[1]],
        out_reduced[:, :inner].T,
        early[:, inner : inner + att_cols],
        early[:, inner + att_cols :],
        out_reduced[:, inner:].T,
        lax.dynamic_slice_in_dim(shared[width : 2 * width], mine, part_rows),
        feed_reduced[:, :ff_local],
        feed_reduced[:, ff_local : 2 * ff_local],
        feed_reduced[:, 2 * ff_local :].T,
    )


def solution(mesh):
    return jax.shard_map(
        local,
        mesh=mesh,
        in_specs=(
            P(None, ("weight", "context"), None),
            P(None, ("weight", "context"), None),
            P("weight"),
            P("weight", "tensor"),
            P("weight", "tensor"),
            P("weight", None),
            P("weight", "tensor"),
            P(None, "tensor"),
            P(),
            P("tensor"),
            P("tensor"),
            P("tensor"),
            P("tensor"),
            P("tensor", "weight"),
            P("weight", "tensor"),
            P("weight", None),
            P("tensor", "weight"),
            P("weight"),
            P("weight", "tensor"),
            P("weight", "tensor"),
            P("tensor", "weight"),
        ),
        out_specs=(
            P(None, ("weight", "context"), None),
            P(None, ("weight", "context"), None),
            P("weight"),
            P("weight", "tensor"),
            P("weight", "tensor"),
            P("weight", None),
            P("weight", "tensor"),
            P(None, "tensor"),
            P(),
            P("tensor"),
            P("tensor"),
            P("tensor"),
            P("tensor"),
            P("tensor", "weight"),
            P("weight", "tensor"),
            P("weight", None),
            P("tensor", "weight"),
            P("weight"),
            P("weight", "tensor"),
            P("weight", "tensor"),
            P("tensor", "weight"),
        ),
        check_vma=False,
    )
```
